768 devices in a mesh: energy: 32 (over y, x), slab: 24 (over z, core).
Axes of the slice: x: 4, y: 8, z: 12, core: 2. Of those that a mesh axis runs over, the one named last changes fastest.
Arguments:
- g_lesser: bfloat16 [32, 24, 320, 640], P('energy', 'slab'), may hold values from -6 to 6
- g_retarded: bfloat16 [32, 24, 320, 640], P('energy', 'slab'), may hold values from -0.25 to 0.25
- screened: bfloat16 [32, 24, 320, 640], P(None, 'slab', 'energy'), may hold values from -1 to 1
- coupling: bfloat16 [24, 320, 320], P('slab'), may hold values from -1.5 to 1.5, as said below
Outputs:
- correction: bfloat16 [32, 24, 320, 640], P('energy', 'slab')
The draws below stay inside these ranges and needn't reach their ends.
Inputs may be any that keep to these rules, and one draw needn't show every extreme that they name: `coupling`: coupling_s is the diagonal entries between 0.75 and 1 plus independent small entries.
All inputs are finite; a program needn't handle non-finite values.
Results may differ from the reference program's by a relative error of at most 0.02.
Values may be sent and summed in bfloat16 or wider, within the bound.
A program may use at most 64 MiB of HBM per device.

```python
import jax
import jax.numpy as jnp
from jax import lax

B = 320
NE = 32
SLABS = 24


def draw_coupling(key, part):
    first = jax.random.fold_in(key, 11)
    second = jax.random.fold_in(key, 12)
    diagonal = jax.random.uniform(first, (SLABS, B), jnp.float32, 0.75, 1.0)
    spread = jnp.clip(jax.random.normal(second, (SLABS, B, B), jnp.float32), -4.0, 4.0) * (0.3 / jnp.sqrt(jnp.float32(B)))
    matrix = spread + jnp.eye(B, dtype=jnp.float32)[None] * diagonal[:, :, None]
    return matrix.astype(jnp.bfloat16)


def block_levels(own_key, extent, cuts, least, top_value):
    def one(axis_at, blocks):
        heights = jax.random.uniform(jax.random.fold_in(jax.random.fold_in(own_key, 6), axis_at), (blocks,), jnp.float32, least / len(cuts), top_value / len(cuts))
        return jnp.repeat(jnp.exp(heights), extent[axis_at] // blocks).reshape((-1,) + (1,) * (len(extent) - axis_at - 1))

    loudness = one(*cuts[0])
    for cut in cuts[1:]:
        loudness = loudness * one(*cut)
    return loudness


def gaussian(key, dims, scale, reach, split=(), kind=jnp.bfloat16):
    factor_of = block_levels(key, dims, split, -0.22, 0.18) if split else 1.0
    array = jax.random.normal(key, dims, jnp.float32) * scale * factor_of
    return jnp.minimum(jnp.maximum(array, -reach), reach).astype(kind)


def setup_inputs(seed: int = 0) -> dict:
    key_of = jax.random.split(jax.random.key(seed), 5)
    return {
        "g_lesser": gaussian(key_of[0], (NE, SLABS, B, 2 * B), 1.0, 6.0, ((0, 32), (1, 24))),
        "g_retarded": gaussian(key_of[1], (NE, SLABS, B, 2 * B), (2 * B) ** -0.5, 0.25, ((0, 32), (1, 24))),
        "screened": gaussian(key_of[2], (NE, SLABS, B, 2 * B), NE ** -0.5, 1.0, ((1, 24), (2, 32))),
        "coupling": draw_coupling(jax.random.fold_in(key_of[4], 71), 0),
    }


def convolve(lesser, screened):
    half = lesser.shape[-1] // 2
    count = lesser.shape[0]
    grid = lesser.astype(jnp.float32)
    inter = screened.astype(jnp.float32)
    lesser_c = grid[..., :half] + 1j * grid[..., half:]
    inter_c = inter[..., :half] + 1j * inter[..., half:]
    length = 2 * count
    product = jnp.fft.fft(lesser_c, n=length, axis=0) * jnp.fft.fft(inter_c, n=length, axis=0)
    conv = jnp.fft.ifft(product, axis=0)[:count]
    return jnp.concatenate([-conv.imag, conv.real], axis=-1).astype(jnp.bfloat16)


def transport(coupling, state):
    count = state.shape[0]
    half = state.shape[-1] // 2
    left = jnp.einsum("ab,nbc->nac", coupling.astype(jnp.float32), state.astype(jnp.float32)).astype(jnp.bfloat16)
    parts = left.reshape(count, half, 2, half)
    moved = jnp.einsum("nakb,cb->nakc", parts.astype(jnp.float32), coupling.astype(jnp.float32))
    return moved.reshape(count, half, 2 * half)


def sandwich(green, state):
    half = green.shape[-1] // 2
    green_re = green[..., :half]
    green_im = green[..., half:]
    state_re = state[..., :half]
    state_im = state[..., half:]
    right_mat = jnp.concatenate([jnp.concatenate([state_re, state_im], -1), jnp.concatenate([-state_im, state_re], -1)], 1)
    left = jnp.einsum("nab,nbc->nac", green.astype(jnp.float32), right_mat.astype(jnp.float32)).astype(jnp.bfloat16)
    tr_re = jnp.swapaxes(green_re, 1, 2)
    tr_im = jnp.swapaxes(green_im, 1, 2)
    adjoint = jnp.concatenate([jnp.concatenate([tr_re, -tr_im], -1), jnp.concatenate([tr_im, tr_re], -1)], 1)
    return jnp.einsum("nab,nbc->nac", left.astype(jnp.float32), adjoint.astype(jnp.float32)).astype(jnp.bfloat16)


def reference(g_lesser, g_retarded, screened, coupling):
    def slab_step(state, index):
        lesser = lax.dynamic_index_in_dim(g_lesser, index, 1, keepdims=False)
        inter = lax.dynamic_index_in_dim(screened, index, 1, keepdims=False)
        green = lax.dynamic_index_in_dim(g_retarded, index, 1, keepdims=False)
        link = lax.dynamic_index_in_dim(coupling, index, 0, keepdims=False)
        sigma = convolve(lesser, inter)
        fresh = sigma.astype(jnp.float32) + transport(link, state.astype(jnp.bfloat16))
        return fresh, sandwich(green, fresh.astype(jnp.bfloat16))

    start = jnp.zeros((NE, B, 2 * B), jnp.float32)
    final, blocks = lax.scan(slab_step, start, jnp.arange(SLABS, dtype=jnp.int32))
    return jnp.swapaxes(blocks, 0, 1)
```

```python
import functools
import math

import jax
import jax.numpy as jnp
from jax import lax
from jax.experimental import pallas as pl
from jax.experimental.pallas import tpu as pltpu
from jax.sharding import PartitionSpec as P

MESH = pl.DeviceIdType.MESH
BF = jnp.bfloat16
F32 = jnp.float32
STARTS = (0, 2, 5, 8)
CHUNKS = 5


def spectral(owned, inter):
    count = owned.shape[0]
    half = owned.shape[-1] // 2
    rows = owned.shape[2]
    length = 2 * count
    freq = jnp.arange(length, dtype=jnp.int32)[:, None]
    point = jnp.arange(count, dtype=jnp.int32)[None, :]
    phase = (freq * point % length).astype(jnp.float32) * (2.0 * math.pi / length)
    fwd_re = jnp.cos(phase)
    fwd_im = -jnp.sin(phase)
    inv_re = jnp.cos(phase).T / length
    inv_im = jnp.sin(phase).T / length
    exact = lax.Precision.HIGHEST

    def forward(block):
        values = block.astype(jnp.float32)
        part_re = values[..., :half].reshape(count, -1)
        part_im = values[..., half:].reshape(count, -1)
        out_re = jnp.dot(fwd_re, part_re, precision=exact) - jnp.dot(
            fwd_im, part_im, precision=exact
        )
        out_im = jnp.dot(fwd_re, part_im, precision=exact) + jnp.dot(
            fwd_im, part_re, precision=exact
        )
        return (out_re, out_im)

    lesser_re, lesser_im = forward(owned)
    inter_re, inter_im = forward(inter)
    prod_re = lesser_re * inter_re - lesser_im * inter_im
    prod_im = lesser_re * inter_im + lesser_im * inter_re
    conv_re = jnp.dot(inv_re, prod_re, precision=exact) - jnp.dot(inv_im, prod_im, precision=exact)
    conv_im = jnp.dot(inv_re, prod_im, precision=exact) + jnp.dot(inv_im, prod_re, precision=exact)
    shape = (count, owned.shape[1], rows, half)
    return jnp.concatenate([-conv_im.reshape(shape), conv_re.reshape(shape)], axis=-1).astype(
        jnp.bfloat16
    )


def nn(a, b):
    return jnp.dot(a, b, preferred_element_type=F32)


def nt(a, b):
    return lax.dot_general(a, b, (((1,), (1,)), ((), ())), preferred_element_type=F32)


def one_of(value, options):
    hit = value == options[0]
    for option in options[1:]:
        hit = jnp.logical_or(hit, value == option)
    return hit


def remote(src, dst, sems, slot, slab):
    return pltpu.make_async_remote_copy(
        src_ref=src,
        dst_ref=dst,
        send_sem=sems.at[0, slot],
        recv_sem=sems.at[1, slot],
        device_id={"slab": slab},
        device_id_type=MESH,
    )


def scan_kernel(
    chips, sig_ref, link_ref, green_ref, out_ref,
    cbuf, abuf, pin, p1, p0, lin, lout, xin, xout, l1, l0, st, xb, sems,
):
    slab = lax.axis_index("slab")
    z = slab // 2
    c = slab % 2
    half = link_ref.shape[0]
    other = 2 * z + 1 - c
    up = slab + 2
    down = slab - 2
    has_up = z < chips - 1
    has_down = z > 0
    start = one_of(z, STARTS)
    end = one_of(z, tuple(s - 1 for s in STARTS[1:]) + (chips - 1,))
    carried = z >= STARTS[1]

    barrier = pltpu.get_barrier_semaphore()
    pl.semaphore_signal(barrier, inc=1, device_id={"slab": other}, device_id_type=MESH)

    @pl.when(has_up)
    def _():
        pl.semaphore_signal(barrier, inc=1, device_id={"slab": up}, device_id_type=MESH)

    @pl.when(has_down)
    def _():
        pl.semaphore_signal(barrier, inc=1, device_id={"slab": down}, device_id_type=MESH)

    pl.semaphore_wait(barrier, 1 + has_up.astype(jnp.int32) + has_down.astype(jnp.int32))

    send_c = remote(link_ref, cbuf.at[c], sems, 0, other)
    send_c.start()
    send_a = remote(sig_ref.at[1 - c], abuf.at[c], sems, 1, other)
    send_a.start()
    cbuf[c] = link_ref[...]
    abuf[c] = sig_ref[c]

    remote(link_ref, cbuf.at[1 - c], sems, 0, other).wait_recv()
    c0 = cbuf[0]
    c1 = cbuf[1]
    pair = nn(c1, c0).astype(BF)

    send_p = remote(p1, pin, sems, 2, up)

    @pl.when(start)
    def _():
        p1[...] = pair
        p0[...] = c0

    @pl.when(jnp.logical_not(start))
    def _():
        remote(p1, pin, sems, 2, up).wait_recv()
        p1[...] = nn(pair, pin[...]).astype(BF)
        p0[...] = nn(c0, pin[...]).astype(BF)

    @pl.when(jnp.logical_not(end))
    def _():
        send_p.start()

    remote(link_ref, abuf.at[1 - c], sems, 1, other).wait_recv()
    a0 = abuf[0]
    mid = nn(c1, a0).astype(BF)
    l1[...] = abuf[1].astype(F32) + nt(mid, c1)
    l0[...] = a0.astype(F32)

    send_l = remote(lout, lin, sems, 3, up)

    @pl.when(jnp.logical_not(start))
    def _():
        send_l.wait_recv()
        before = lin[...]
        l1[...] += nn(pair, nt(before, pair).astype(BF))

    @pl.when(jnp.logical_not(end))
    def _():
        lout[...] = l1[...].astype(BF)
        send_l.start()

    @pl.when(jnp.logical_not(start))
    def _():
        l0[...] += nn(c0, nt(lin[...], c0).astype(BF))

    depth = half // CHUNKS

    def carry(k, src):
        rows = pl.ds(k * depth, depth)
        return remote(src.at[rows, :], xin.at[rows, :], sems, 4 + k, up)

    @pl.when(carried)
    def _():
        for k in range(CHUNKS):
            carry(k, xin).wait_recv()

            @pl.when(jnp.logical_not(end))
            def _():
                carry(k, xin).start()

        before = xin[...]
        l1[...] += nn(p1[...], nt(before, p1[...]).astype(BF))

    @pl.when(jnp.logical_and(end, has_up))
    def _():
        xout[...] = l1[...].astype(BF)
        for k in range(CHUNKS):
            carry(k, xout).start()

    @pl.when(carried)
    def _():
        l0[...] += nn(p0[...], nt(xin[...], p0[...]).astype(BF))

    st[0] = l0[...].astype(BF)
    st[1] = l1[...].astype(BF)
    send_x = remote(st.at[1 - c], xb.at[c], sems, 4 + CHUNKS, other)
    send_x.start()
    xb[c] = st[c]

    green_re = green_ref[:, :half]
    green_im = green_ref[:, half:]

    remote(st.at[1 - c], xb.at[1 - c], sems, 4 + CHUNKS, other).wait_recv()
    x_re = xb[0]
    x_im = xb[1]
    left_re = (nn(green_re, x_re) - nn(green_im, x_im)).astype(BF)
    left_im = (nn(green_re, x_im) + nn(green_im, x_re)).astype(BF)
    cor_re = nt(left_re, green_re) + nt(left_im, green_im)
    cor_im = nt(left_im, green_re) - nt(left_re, green_im)
    out_ref[...] = jnp.concatenate([cor_re, cor_im], axis=1).astype(BF)

    send_c.wait_send()
    send_a.wait_send()
    send_x.wait_send()

    @pl.when(jnp.logical_not(end))
    def _():
        send_p.wait_send()
        send_l.wait_send()

    @pl.when(jnp.logical_or(jnp.logical_and(carried, has_up), end & has_up))
    def _():
        for k in range(CHUNKS):
            carry(k, xin).wait_send()


def scan(chips, sigma, link, green):
    half = link.shape[0]
    square = (half, half)
    vmem = pl.BlockSpec(memory_space=pltpu.VMEM)
    return pl.pallas_call(
        functools.partial(scan_kernel, chips),
        out_shape=jax.ShapeDtypeStruct((half, 2 * half), BF),
        in_specs=[vmem] * 3,
        out_specs=vmem,
        scratch_shapes=[
            pltpu.VMEM((2,) + square, BF),
            pltpu.VMEM((2,) + square, BF),
            pltpu.VMEM(square, BF),
            pltpu.VMEM(square, BF),
            pltpu.VMEM(square, BF),
            pltpu.VMEM(square, BF),
            pltpu.VMEM(square, BF),
            pltpu.VMEM(square, BF),
            pltpu.VMEM(square, BF),
            pltpu.VMEM(square, F32),
            pltpu.VMEM(square, F32),
            pltpu.VMEM((2,) + square, BF),
            pltpu.VMEM((2,) + square, BF),
            pltpu.SemaphoreType.DMA((2, 5 + CHUNKS)),
        ],
        compiler_params=pltpu.CompilerParams(
            collective_id=0, has_side_effects=True, vmem_limit_bytes=40 << 20
        ),
    )(sigma, link, green)


def solution(mesh):
    chips = mesh.shape["slab"] // 2

    def local(g_lesser, g_retarded, screened, coupling):
        owned = lax.all_to_all(g_lesser, "energy", split_axis=2, concat_axis=0, tiled=True)
        sigma_rows = spectral(owned, screened)
        sigma = lax.all_to_all(sigma_rows, "energy", split_axis=0, concat_axis=2, tiled=True)[0, 0]
        half = sigma.shape[-1] // 2
        streams = jnp.stack([sigma[:, :half], sigma[:, half:]])
        return scan(chips, streams, coupling[0], g_retarded[0, 0])[None, None]

    placed = (
        P("energy", "slab", None, None),
        P("energy", "slab", None, None),
        P(None, "slab", "energy", None),
        P("slab", None, None),
    )
    return jax.shard_map(
        local,
        mesh=mesh,
        in_specs=placed,
        out_specs=P("energy", "slab", None, None),
        check_vma=False,
    )
```
